32 devices in a mesh: blk: 16 (over z, y, core), uly: 2 (over x).
Axes of the slice: x: 2, y: 2, z: 4, core: 2. Of those that a mesh axis runs over, the one named last changes fastest.
Arguments:
- queries: bfloat16 [8192, 6144], P(('blk', 'uly')), may hold values from -8 to 8
- keys: bfloat16 [2048, 6144], P(('blk', 'uly')), may hold values from -8 to 8
- values: bfloat16 [2048, 6144], P(('blk', 'uly')), may hold values from -6 to 6
- block_lists: int32 [48, 64, 16], replicated, may hold values from 0 to 15, as said below
- block_counts: int32 [48, 64], replicated, may hold values from 1 to 16, as said below
Outputs:
- attended: bfloat16 [8192, 6144], P(('blk', 'uly'))
The draws below stay inside these ranges and needn't reach their ends.
Inputs may be any that keep to these rules, and one draw needn't show every extreme that they name: `block_lists`: entry 0 of the list for query block a is always the key block at the same relative place in the sequence, the integer part of a times 16 divided by 64; the first block_counts entries of a list are distinct key blocks; entries after them are key block numbers that are ignored. `block_counts`: counts differ widely from head to head.
All inputs are finite; a program needn't handle non-finite values.
Results may differ from the reference program's by a relative error of at most 0.0055.
Values may be sent and summed in bfloat16 or wider, within the bound.
A program may use at most 256 MiB of HBM per device.

```python
import math
import jax
import jax.numpy as jnp
from jax import lax

HEADS = 48
HEAD_DIM = 128
D = 6144
BLOCK = 128
SEL_MAX = 16
QBLOCKS = 64
KBLOCKS = 16
QTOKENS = 8192
KTOKENS = 2048


def draw_queries(key, part):
    drawn = jax.random.normal(jax.random.fold_in(key, 1), (QTOKENS, D), jnp.float32)
    return jnp.clip(drawn, -8.0, 8.0).astype(jnp.bfloat16)


def draw_keys(key, part):
    drawn = jax.random.normal(jax.random.fold_in(key, 3), (KTOKENS, D), jnp.float32)
    return jnp.clip(drawn, -8.0, 8.0).astype(jnp.bfloat16)


def selection(key):
    per_head = jax.random.randint(jax.random.fold_in(key, 21), (HEADS,), 1, SEL_MAX + 1)
    jitter = jax.random.randint(jax.random.fold_in(key, 22), (HEADS, QBLOCKS), -1, 2)
    counts = jnp.clip(per_head[:, None] + jitter, 1, SEL_MAX)
    heavy = jax.random.randint(jax.random.fold_in(key, 23), (), 0, HEADS)
    counts = counts.at[heavy, 0].set(SEL_MAX)
    counts = counts.at[(heavy + 1) % HEADS, 0].set(1)
    tile_keys = jax.random.split(jax.random.fold_in(key, 24), HEADS * QBLOCKS)
    others = jax.vmap(lambda single: jax.random.permutation(single, KBLOCKS - 1)[:SEL_MAX - 1])(tile_keys)
    others = others.reshape(HEADS, QBLOCKS, SEL_MAX - 1).astype(jnp.int32)
    diagonal = (jnp.arange(QBLOCKS, dtype=jnp.int32) * KBLOCKS // QBLOCKS)[None, :, None]
    others = others + (others >= diagonal).astype(jnp.int32)
    leading = jnp.broadcast_to(diagonal, (HEADS, QBLOCKS, 1))
    lists = jnp.concatenate([leading, others], axis=2).astype(jnp.int32)
    return (lists, counts.astype(jnp.int32))


def draw_block_lists(key, part):
    return selection(key)[0]


def draw_block_counts(key, part):
    return selection(key)[1]


def steps_of(stream_key, shape, cuts, least, high):
    level = 1.0
    for axis_at, shards_of in cuts:
        heights = jax.random.uniform(jax.random.fold_in(jax.random.fold_in(stream_key, 6), axis_at), (shards_of,), jnp.float32, least / len(cuts), high / len(cuts))
        level = level * jnp.repeat(jnp.exp(heights), shape[axis_at] // shards_of).reshape((-1,) + (1,) * (len(shape) - 1 - axis_at))
    return level


def scatter_about(rng, shape, deviation, most, pieces=(), kind=jnp.bfloat16):
    entries = deviation * jax.random.normal(rng, shape, jnp.float32)
    if pieces:
        entries = entries * steps_of(rng, shape, pieces, -0.22, 0.18)
    return jnp.clip(entries, -most, most).astype(kind)


def setup_inputs(seed: int = 0) -> dict:
    key_of = jax.random.split(jax.random.key(seed), 6)
    queries = draw_queries(jax.random.fold_in(key_of[5], 71), 0)
    keys = draw_keys(jax.random.fold_in(key_of[5], 71), 0)
    values = scatter_about(key_of[2], (KTOKENS, D), 1.0, 6.0, ((0, 32),))
    block_lists = draw_block_lists(jax.random.fold_in(key_of[5], 71), 0)
    block_counts = draw_block_counts(jax.random.fold_in(key_of[5], 71), 0)
    return {"queries": queries, "keys": keys, "values": values, "block_lists": block_lists, "block_counts": block_counts}


NEGATIVE = -1e+30

def reference(queries, keys, values, block_lists, block_counts):
    scaling = 1.0 / math.sqrt(HEAD_DIM)

    def one_tile(position):
        head_index = position // QBLOCKS
        query_block = position % QBLOCKS
        query_rows = lax.dynamic_slice(queries, (query_block * BLOCK, head_index * HEAD_DIM), (BLOCK, HEAD_DIM)).astype(jnp.float32)
        listed = block_lists[head_index, query_block]
        count_used = block_counts[head_index, query_block]

        def fetch(block_number):
            first = (block_number * BLOCK).astype(jnp.int32)
            column = (head_index * HEAD_DIM).astype(jnp.int32)
            key_tile = lax.dynamic_slice(keys, (first, column), (BLOCK, HEAD_DIM))
            value_tile = lax.dynamic_slice(values, (first, column), (BLOCK, HEAD_DIM))
            return (key_tile, value_tile)
        key_tiles, value_tiles = jax.vmap(fetch)(listed)
        key_flat = key_tiles.reshape(SEL_MAX * BLOCK, HEAD_DIM).astype(jnp.float32)
        value_flat = value_tiles.reshape(SEL_MAX * BLOCK, HEAD_DIM).astype(jnp.float32)
        scores = jnp.einsum('qd,kd->qk', query_rows, key_flat) * scaling
        usable = jnp.repeat(jnp.arange(SEL_MAX, dtype=jnp.int32) < count_used, BLOCK)[None, :]
        top = lax.optimization_barrier(jnp.max(jnp.where(usable, scores, NEGATIVE), axis=1))
        weights = jnp.where(usable, jnp.exp(scores - top[:, None]), 0.0)
        total = lax.optimization_barrier(jnp.sum(weights, axis=1))
        rounded = lax.optimization_barrier(weights.astype(jnp.bfloat16)).astype(jnp.float32)
        mixed = jnp.einsum('qk,kd->qd', rounded, value_flat) / total[:, None]
        return mixed.astype(jnp.bfloat16)
    tiles = lax.map(one_tile, jnp.arange(HEADS * QBLOCKS, dtype=jnp.int32))
    tiles = tiles.reshape(HEADS, QBLOCKS * BLOCK, HEAD_DIM)
    return jnp.transpose(tiles, (1, 0, 2)).reshape(QBLOCKS * BLOCK, HEADS * HEAD_DIM)
```

```python
import functools
import math

import jax
import jax.numpy as jnp
from jax import lax
from jax.experimental import pallas as pl
from jax.experimental.pallas import tpu as pltpu
from jax.sharding import PartitionSpec as P

HEAD_DIM = 128
BLOCK = 128
NEGATIVE = -1e30
MESH = pl.DeviceIdType.MESH


def attend_kernel(
    blk_n, uly_n, group, q_any, k_any, v_any, bias_ref, o_any,
    qbuf, kbuf, vbuf, obuf,
    kv_send, k_recv, v_recv, q_send, q_recv, o_send, o_recv, local_sem,
):
    devices = blk_n * uly_n
    me = lax.axis_index("blk") * uly_n + lax.axis_index("uly")
    first = (me // group) * group
    place = me - first
    rows = q_any.shape[0]
    width = qbuf.shape[2]
    heads = width // HEAD_DIM
    keys_all = kbuf.shape[0] * kbuf.shape[1]
    qblocks = bias_ref.shape[1]
    scaling = 1.0 / math.sqrt(HEAD_DIM)

    def coords(device):
        return (device // uly_n, lax.rem(device, uly_n))

    def columns(position):
        return pl.ds(pl.multiple_of(position * width, HEAD_DIM), width)

    own = (
        pltpu.make_async_copy(k_any.at[:, columns(place)], kbuf.at[me], local_sem.at[0]),
        pltpu.make_async_copy(v_any.at[:, columns(place)], vbuf.at[me], local_sem.at[1]),
        pltpu.make_async_copy(q_any.at[:, columns(place)], qbuf.at[place], local_sem.at[2]),
    )
    for copy in own:
        copy.start()

    barrier = pltpu.get_barrier_semaphore()

    def greet(step, carry):
        other = lax.rem(me + step, devices)
        pl.semaphore_signal(barrier, inc=1, device_id=coords(other), device_id_type=MESH)
        return carry

    lax.fori_loop(1, devices, greet, 0)
    pl.semaphore_wait(barrier, devices - 1)

    def send_kv(step, carry):
        other = lax.rem(me + devices - step, devices)
        cols = columns(lax.rem(other, group))
        pltpu.make_async_remote_copy(
            src_ref=k_any.at[:, cols], dst_ref=kbuf.at[me],
            send_sem=kv_send.at[0], recv_sem=k_recv,
            device_id=coords(other), device_id_type=MESH,
        ).start()
        pltpu.make_async_remote_copy(
            src_ref=v_any.at[:, cols], dst_ref=vbuf.at[me],
            send_sem=kv_send.at[1], recv_sem=v_recv,
            device_id=coords(other), device_id_type=MESH,
        ).start()
        return carry

    lax.fori_loop(1, devices, send_kv, 0)

    def send_q(step, carry):
        there = lax.rem(place + group - step, group)
        pltpu.make_async_remote_copy(
            src_ref=q_any.at[:, columns(there)], dst_ref=qbuf.at[place],
            send_sem=q_send, recv_sem=q_recv.at[place],
            device_id=coords(first + there), device_id_type=MESH,
        ).start()
        return carry

    lax.fori_loop(1, group, send_q, 0)

    for copy in own:
        copy.wait()
    rest = pl.ds(0, devices - 1)
    pltpu.make_async_copy(kbuf.at[rest], kbuf.at[rest], k_recv).wait()
    pltpu.make_async_copy(vbuf.at[rest], vbuf.at[rest], v_recv).wait()

    def attend(source):
        for head in range(heads):
            cols = slice(head * HEAD_DIM, (head + 1) * HEAD_DIM)
            query = qbuf[source, :, cols]
            key = kbuf[:, :, cols].reshape(keys_all, HEAD_DIM)
            value = vbuf[:, :, cols].reshape(keys_all, HEAD_DIM)
            scores = lax.dot_general(
                query, key, (((1,), (1,)), ((), ())), preferred_element_type=jnp.float32
            )
            if rows >= BLOCK:
                count = rows // BLOCK
                parts = [
                    scores[b * BLOCK : (b + 1) * BLOCK]
                    + bias_ref[head, pl.ds(source * count + b, 1), :]
                    for b in range(count)
                ]
                scores = jnp.concatenate(parts, axis=0)
            else:
                scores = scores + bias_ref[head, pl.ds((source * rows) // BLOCK, 1), :]
            top = jnp.max(scores, axis=1, keepdims=True)
            weights = jnp.exp((scores - top) * scaling)
            total = jnp.sum(weights, axis=1, keepdims=True)
            mixed = jnp.dot(
                weights.astype(jnp.bfloat16), value, preferred_element_type=jnp.float32
            )
            obuf[source, :, cols] = (mixed / total).astype(jnp.bfloat16)

    attend(place)
    home = pltpu.make_async_copy(
        obuf.at[place], o_any.at[:, columns(place)], local_sem.at[3]
    )
    home.start()

    def visit(step, carry):
        source = lax.rem(place + step, group)
        pltpu.make_async_copy(qbuf.at[source], qbuf.at[source], q_recv.at[source]).wait()
        attend(source)
        pltpu.make_async_remote_copy(
            src_ref=obuf.at[source], dst_ref=o_any.at[:, columns(place)],
            send_sem=o_send, recv_sem=o_recv,
            device_id=coords(first + source), device_id_type=MESH,
        ).start()
        return carry

    lax.fori_loop(1, group, visit, 0)
    home.wait()
    pltpu.make_async_copy(kbuf.at[rest], kbuf.at[rest], kv_send.at[0]).wait()
    pltpu.make_async_copy(vbuf.at[rest], vbuf.at[rest], kv_send.at[1]).wait()
    peers = pl.ds(0, group - 1)
    pltpu.make_async_copy(qbuf.at[peers], qbuf.at[peers], q_send).wait()
    pltpu.make_async_copy(obuf.at[peers], obuf.at[peers], o_send).wait()
    pltpu.make_async_copy(obuf.at[peers], obuf.at[peers], o_recv).wait()


def local(blk_n, uly_n, queries, keys, values, block_lists, block_counts):
    heads_all, qblocks_all, listed = block_lists.shape
    share = math.gcd(blk_n, heads_all // uly_n)
    group = share * uly_n
    heads = heads_all // group
    groups = blk_n // share
    qblocks = qblocks_all // groups
    devices = blk_n * uly_n
    rows, key_rows = queries.shape[0], keys.shape[0]
    width = heads * HEAD_DIM
    keys_all = key_rows * devices

    me = lax.axis_index("blk") * uly_n + lax.axis_index("uly")
    place = lax.rem(me, group)
    lists = lax.dynamic_slice(
        block_lists, (place * heads, (me // group) * qblocks, 0), (heads, qblocks, listed)
    )
    counts = lax.dynamic_slice(
        block_counts, (place * heads, (me // group) * qblocks), (heads, qblocks)
    )
    usable = jnp.arange(listed, dtype=jnp.int32) < counts[:, :, None]
    chosen = jnp.where(usable, lists, -1)
    blocks = jnp.arange(keys_all // BLOCK, dtype=jnp.int32)
    member = jnp.any(chosen[:, :, :, None] == blocks, axis=2)
    bias = jnp.repeat(jnp.where(member, 0.0, NEGATIVE).astype(jnp.float32), BLOCK, axis=2)

    any_spec = pl.BlockSpec(memory_space=pl.ANY)
    dma = pltpu.SemaphoreType.DMA
    return pl.pallas_call(
        functools.partial(attend_kernel, blk_n, uly_n, group),
        out_shape=jax.ShapeDtypeStruct(queries.shape, queries.dtype),
        in_specs=[any_spec, any_spec, any_spec, pl.BlockSpec(memory_space=pltpu.VMEM)],
        out_specs=any_spec,
        scratch_shapes=[
            pltpu.VMEM((group, rows, width), jnp.bfloat16),
            pltpu.VMEM((devices, key_rows, width), jnp.bfloat16),
            pltpu.VMEM((devices, key_rows, width), jnp.bfloat16),
            pltpu.VMEM((group, rows, width), jnp.bfloat16),
            dma((2,)), dma, dma, dma, dma((group,)), dma, dma, dma((4,)),
        ],
        compiler_params=pltpu.CompilerParams(
            collective_id=0, has_side_effects=True, vmem_limit_bytes=60 * 1024 * 1024
        ),
    )(queries, keys, values, bias)


def solution(mesh):
    return jax.shard_map(
        functools.partial(local, mesh.shape["blk"], mesh.shape["uly"]),
        mesh=mesh,
        in_specs=(
            P(("blk", "uly"), None),
            P(("blk", "uly"), None),
            P(("blk", "uly"), None),
            P(),
            P(),
        ),
        out_specs=P(("blk", "uly"), None),
        check_vma=False,
    )
```

```python
import functools
import math

import jax
import jax.numpy as jnp
from jax import lax
from jax.experimental import pallas as pl
from jax.experimental.pallas import tpu as pltpu
from jax.sharding import PartitionSpec as P

HEAD_DIM = 128
BLOCK = 128
NEGATIVE = -1e30
MESH = pl.DeviceIdType.MESH


def mix(a, b, n):
    if n & (n - 1):
        return lax.rem(n + b - a, n)
    out, bit = 0, 1
    while bit < n:
        out = out + lax.rem(a // bit + b // bit, 2) * bit
        bit *= 2
    return out


def attend_kernel(
    blk_n, uly_n, group, q_any, k_any, v_any, bias_ref, o_any,
    qbuf, kbuf, vbuf, obuf, hot,
    kv_send, k_recv, v_recv, q_send, q_recv, o_send, o_recv, local_sem,
):
    devices = blk_n * uly_n
    me = lax.axis_index("blk") * uly_n + lax.axis_index("uly")
    first = (me // group) * group
    place = me - first
    rows = q_any.shape[0]
    width = qbuf.shape[2]
    heads = width // HEAD_DIM
    keys_all = kbuf.shape[0] * kbuf.shape[1]
    flags = bias_ref.shape[2]
    scaling = math.log2(math.e) / math.sqrt(HEAD_DIM)

    def coords(device):
        return (device // uly_n, lax.rem(device, uly_n))

    def columns(position):
        return pl.ds(pl.multiple_of(position * width, HEAD_DIM), width)

    own = (
        pltpu.make_async_copy(k_any.at[:, columns(place)], kbuf.at[me], local_sem.at[0]),
        pltpu.make_async_copy(v_any.at[:, columns(place)], vbuf.at[me], local_sem.at[1]),
        pltpu.make_async_copy(q_any.at[:, columns(place)], qbuf.at[place], local_sem.at[2]),
    )
    for copy in own:
        copy.start()

    barrier = pltpu.get_barrier_semaphore()

    def greet(step, carry):
        other = lax.rem(me + step, devices)
        pl.semaphore_signal(barrier, inc=1, device_id=coords(other), device_id_type=MESH)
        return carry

    lax.fori_loop(1, devices, greet, 0)
    pl.semaphore_wait(barrier, devices - 1)

    def send_kv(step, carry):
        other = mix(me, step, devices)
        cols = columns(lax.rem(other, group))
        pltpu.make_async_remote_copy(
            src_ref=k_any.at[:, cols], dst_ref=kbuf.at[me],
            send_sem=kv_send.at[0], recv_sem=k_recv,
            device_id=coords(other), device_id_type=MESH,
        ).start()
        pltpu.make_async_remote_copy(
            src_ref=v_any.at[:, cols], dst_ref=vbuf.at[me],
            send_sem=kv_send.at[1], recv_sem=v_recv,
            device_id=coords(other), device_id_type=MESH,
        ).start()
        return carry

    lax.fori_loop(1, devices, send_kv, 0)

    def send_q(step, carry):
        there = mix(place, step, group)
        pltpu.make_async_remote_copy(
            src_ref=q_any.at[:, columns(there)], dst_ref=qbuf.at[place],
            send_sem=q_send, recv_sem=q_recv.at[place],
            device_id=coords(first + there), device_id_type=MESH,
        ).start()
        return carry

    lax.fori_loop(1, group, send_q, 0)

    key_block = lax.broadcasted_iota(jnp.int32, hot.shape, 0) // BLOCK
    lane = lax.broadcasted_iota(jnp.int32, hot.shape, 1)
    hot[...] = jnp.where(key_block == lane, 1.0, 0.0).astype(jnp.bfloat16)

    for copy in own:
        copy.wait()
    rest = pl.ds(0, devices - 1)
    pltpu.make_async_copy(kbuf.at[rest], kbuf.at[rest], k_recv).wait()
    pltpu.make_async_copy(vbuf.at[rest], vbuf.at[rest], v_recv).wait()

    def attend(source):
        for head in range(heads):
            cols = slice(head * HEAD_DIM, (head + 1) * HEAD_DIM)
            spans = max(rows // BLOCK, 1)
            flag = [
                jnp.broadcast_to(
                    bias_ref[head, pl.ds((source * rows) // BLOCK + b, 1), :],
                    (rows // spans, flags),
                ).astype(jnp.bfloat16)
                for b in range(spans)
            ]
            query = jnp.concatenate([qbuf[source, :, cols], jnp.concatenate(flag, axis=0)], axis=1)
            key = jnp.concatenate(
                [kbuf[:, :, cols].reshape(keys_all, HEAD_DIM), hot[...]], axis=1
            )
            value = vbuf[:, :, cols].reshape(keys_all, HEAD_DIM)
            scores = lax.dot_general(
                query, key, (((1,), (1,)), ((), ())), preferred_element_type=jnp.float32
            )
            top = jnp.max(scores, axis=1, keepdims=True)
            weights = jnp.exp2((scores - top) * scaling)
            total = jnp.sum(weights, axis=1, keepdims=True)
            mixed = jnp.dot(
                weights.astype(jnp.bfloat16), value, preferred_element_type=jnp.float32
            )
            obuf[source, :, cols] = (mixed / total).astype(jnp.bfloat16)

    attend(place)
    home = pltpu.make_async_copy(
        obuf.at[place], o_any.at[:, columns(place)], local_sem.at[3]
    )
    home.start()

    def visit(step, carry):
        source = mix(place, step, group)
        pltpu.make_async_copy(qbuf.at[source], qbuf.at[source], q_recv.at[source]).wait()
        attend(source)
        pltpu.make_async_remote_copy(
            src_ref=obuf.at[source], dst_ref=o_any.at[:, columns(place)],
            send_sem=o_send, recv_sem=o_recv,
            device_id=coords(first + source), device_id_type=MESH,
        ).start()
        return carry

    lax.fori_loop(1, group, visit, 0)
    home.wait()
    pltpu.make_async_copy(kbuf.at[rest], kbuf.at[rest], kv_send.at[0]).wait()
    pltpu.make_async_copy(vbuf.at[rest], vbuf.at[rest], kv_send.at[1]).wait()
    peers = pl.ds(0, group - 1)
    pltpu.make_async_copy(qbuf.at[peers], qbuf.at[peers], q_send).wait()
    pltpu.make_async_copy(obuf.at[peers], obuf.at[peers], o_send).wait()
    pltpu.make_async_copy(obuf.at[peers], obuf.at[peers], o_recv).wait()


def local(blk_n, uly_n, queries, keys, values, block_lists, block_counts):
    heads_all, qblocks_all, listed = block_lists.shape
    share = math.gcd(blk_n, heads_all // uly_n)
    group = share * uly_n
    heads = heads_all // group
    groups = blk_n // share
    qblocks = qblocks_all // groups
    devices = blk_n * uly_n
    rows, key_rows = queries.shape[0], keys.shape[0]
    width = heads * HEAD_DIM
    keys_all = key_rows * devices

    me = lax.axis_index("blk") * uly_n + lax.axis_index("uly")
    place = lax.rem(me, group)
    lists = lax.dynamic_slice(
        block_lists, (place * heads, (me // group) * qblocks, 0), (heads, qblocks, listed)
    )
    counts = lax.dynamic_slice(
        block_counts, (place * heads, (me // group) * qblocks), (heads, qblocks)
    )
    usable = jnp.arange(listed, dtype=jnp.int32) < counts[:, :, None]
    chosen = jnp.where(usable, lists, -1)
    key_blocks = keys_all // BLOCK
    flags = -(-key_blocks // HEAD_DIM) * HEAD_DIM
    blocks = jnp.arange(flags, dtype=jnp.int32)
    member = jnp.any(chosen[:, :, :, None] == blocks, axis=2)
    bias = jnp.where(member, 0.0, NEGATIVE).astype(jnp.float32)

    any_spec = pl.BlockSpec(memory_space=pl.ANY)
    dma = pltpu.SemaphoreType.DMA
    return pl.pallas_call(
        functools.partial(attend_kernel, blk_n, uly_n, group),
        out_shape=jax.ShapeDtypeStruct(queries.shape, queries.dtype),
        in_specs=[any_spec, any_spec, any_spec, pl.BlockSpec(memory_space=pltpu.VMEM)],
        out_specs=any_spec,
        scratch_shapes=[
            pltpu.VMEM((group, rows, width), jnp.bfloat16),
            pltpu.VMEM((devices, key_rows, width), jnp.bfloat16),
            pltpu.VMEM((devices, key_rows, width), jnp.bfloat16),
            pltpu.VMEM((group, rows, width), jnp.bfloat16),
            pltpu.VMEM((keys_all, flags), jnp.bfloat16),
            dma((2,)), dma, dma, dma, dma((group,)), dma, dma, dma((4,)),
        ],
        compiler_params=pltpu.CompilerParams(
            collective_id=0, has_side_effects=True, vmem_limit_bytes=60 * 1024 * 1024
        ),
    )(queries, keys, values, bias)


def solution(mesh):
    return jax.shard_map(
        functools.partial(local, mesh.shape["blk"], mesh.shape["uly"]),
        mesh=mesh,
        in_specs=(
            P(("blk", "uly"), None),
            P(("blk", "uly"), None),
            P(("blk", "uly"), None),
            P(),
            P(),
        ),
        out_specs=P(("blk", "uly"), None),
        check_vma=False,
    )
```
